768 devices in a mesh: sec: 12 (over z), tile: 64 (over y, x, core).
Axes of the slice: x: 4, y: 8, z: 12, core: 2. Of those that a mesh axis runs over, the one named last changes fastest.
Arguments:
- atm_tracers: bfloat16 [2, 128, 96, 8192], P(None, None, 'sec', 'tile'), may hold values from -6 to 6
- atm_courant: bfloat16 [128, 96, 8192], P(None, 'sec', 'tile'), may hold values from -0.69921875 to 0.69921875
- atm_diffusion: float32 [128], replicated, may hold values from 0.02 to 0.15
- ocean_tracers: bfloat16 [2, 80, 96, 8192], P(None, None, 'sec', 'tile'), may hold values from -6 to 6
- ocean_courant: bfloat16 [80, 96, 8192], P(None, 'sec', 'tile'), may hold values from -0.5 to 0.5
- ocean_diffusion: float32 [80], replicated, may hold values from 0.02 to 0.15
- surface_seen: float32 [2, 96, 8192], P(None, 'sec', 'tile'), may hold values from -6 to 6
- bulk_coeff: float32 [96, 8192], P('sec', 'tile'), may hold values from 0.2 to 1
- flux_owner: int32 [12, 64, 8, 1], P('sec', 'tile'), may hold values from 0 to 11; in each aligned block of 8 rows (0 to 7, 8 to 15, ..., all dimensions but the last counted through in order) at most 2 rows name the same one
- flux_slot: int32 [12, 64, 8], P('sec', 'tile'), may hold values from 0 to 7
- flux_weight: float32 [12, 64, 8], P('sec', 'tile'), may hold values from 0.5 to 1.5
- ocean_mask: int32 [96, 8192], P('sec', 'tile'), may hold values 0 or 1
Outputs:
- atm_next: bfloat16 [2, 128, 96, 8192], P(None, None, 'sec', 'tile')
- ocean_next: bfloat16 [2, 80, 96, 8192], P(None, None, 'sec', 'tile')
- surface_next: float32 [2, 96, 8192], P(None, 'sec', 'tile')
The draws below stay inside these ranges and needn't reach their ends.
Inputs may be any that keep to these rules, and one draw needn't show every extreme that they name: `flux_owner`: among the 8 blocks of one device, each owner is named at most 2 times.
All inputs are finite; a program needn't handle non-finite values. No bound on the sum of `ocean_mask` on one device may be relied on, other than what follows from the above.
Results may differ from the reference program's by a relative error of at most 0.0045.
Values may be sent and summed in bfloat16 or wider, within the bound.
A program may use at most 32 MiB of HBM per device.

```python
import math
import jax
import jax.numpy as jnp
import numpy as np
from jax import lax

LEV_ATM = 128
LEV_OCN = 80
ROWS_ATM = 8
ROWS_OCN = 8
STRIP = 128
ATM_STEPS = 3
OCN_STEPS = 2
FLUX_CAP = 2
NROWS_ATM = 96
NROWS_OCN = 96
NCOLS = 8192
N_SEC = 12
N_TILE = 64


def touch_ends(values, stream_key, low, top_value):
    dims = values.shape
    place = [jax.random.randint(jax.random.fold_in(stream_key, axis), (), 0, dims[axis]) for axis in range(len(dims))]
    values = values.at[tuple(place)].set(low)
    longest = dims.index(max(dims))
    place[longest] = (place[longest] + 1) % dims[longest]
    return values.at[tuple(place)].set(top_value)


def steps_of(stream_key, dims, cuts, smallest, high):
    def one(dim, parts):
        draws = jax.random.uniform(jax.random.fold_in(jax.random.fold_in(stream_key, 6), dim), (parts,), jnp.float32, smallest / len(cuts), high / len(cuts))
        return jnp.repeat(jnp.exp(draws), dims[dim] // parts).reshape((-1,) + (1,) * (len(dims) - dim - 1))

    factor_of = one(*cuts[0])
    for cut in cuts[1:]:
        factor_of = factor_of * one(*cut)
    return factor_of


def assign_block(own_key, own, number, rows, count, top, limit, skew):
    sequence = jax.random.permutation(own_key, count)
    packed, common = portions_of(count, rows * top, limit, skew, True), portions_of(count, rows * top, limit, skew, False)
    places = jnp.arange(count)

    def named(tallies, offset_by):
        used = int((tallies > 0).sum())
        fixed = max(1, used // 4)
        passed = fixed + (places - fixed + offset_by * (used - fixed)) % max(1, count - fixed)
        return jnp.zeros((count,), jnp.int32).at[sequence[jnp.where(places < fixed, places, passed)]].set(jnp.asarray(tallies, jnp.int32))

    tallies = jnp.where(number % 4 == 0, named(packed, number // 4), named(common, number - number // 4 - 1))
    mixed = jax.random.permutation(jax.random.fold_in(own, 3), count)
    source_of, receiver = mixed[0:count // 2 * 2:2], mixed[1:count // 2 * 2:2]
    slack = jnp.minimum(tallies[source_of] - 1, limit - tallies[receiver]) // 2
    slack = jnp.where((source_of == sequence[0]) | (receiver == sequence[0]) | (tallies[receiver] == 0), 0, jnp.maximum(slack, 0))
    passed = jax.random.randint(jax.random.fold_in(own, 4), (count // 2,), 0, 1 << 20) % (slack + 1)
    tallies = tallies.at[source_of].add(-passed).at[receiver].add(passed)
    labels = jnp.searchsorted(jnp.cumsum(tallies), jnp.arange(rows * top), side="right").astype(jnp.int32)
    grid = labels.reshape(top, rows).T
    grid = grid[jax.random.permutation(jax.random.fold_in(own, 1), rows)]
    offset_by = jax.random.randint(jax.random.fold_in(own, 2), (rows, 1), 0, top)
    return jnp.take_along_axis(grid, (jnp.arange(top)[None, :] + offset_by) % top, axis=1)


def portions_of(amount, total, most, skew, full):
    weights = [(1 << 20) // math.isqrt(standing ** skew) + 1 for standing in range(1, amount + 1)]
    largest = most if full else min(most, max(-(-total // amount), total * weights[0] // sum(weights)))
    least = 1 if total - largest >= amount - 1 else 0
    counts, spare = [largest] + [least] * (amount - 1), total - largest - least * (amount - 1)
    while spare > 0:
        free = [i for i in range(1, amount) if counts[i] < largest] or [i for i in range(1, amount) if counts[i] < most]
        pool, remaining = sum([weights[i] for i in free]), spare
        for i in free:
            addition = min(most - counts[i], max(1, remaining * weights[i] // pool), spare)
            counts[i] = counts[i] + addition
            spare = spare - addition
    return np.array(counts)


def bell_draw(key, extent, scale, most, cuts=(), held_as=jnp.bfloat16):
    level = steps_of(key, extent, cuts, -0.22, 0.18) if cuts else 1.0
    array = jax.random.normal(key, extent, jnp.float32) * scale * level
    return jnp.minimum(jnp.maximum(array, -most), most).astype(held_as)


def setup_inputs(seed: int = 0) -> dict:
    seeds = jax.random.split(jax.random.key(seed), 13)
    atm_tracers = bell_draw(seeds[0], (2, LEV_ATM, NROWS_ATM, NCOLS), 1.0, 6.0, ((2, 12), (3, 64)))
    atm_courant = jnp.clip(jax.random.uniform(seeds[1], (LEV_ATM, NROWS_ATM, NCOLS), jnp.float32, -0.69921875, 0.69921875) * steps_of(seeds[1], (LEV_ATM, NROWS_ATM, NCOLS), ((1, 12), (2, 64)), -0.4, 0.0), -0.69921875, 0.69921875).astype(jnp.bfloat16)
    atm_diffusion = jnp.clip(jnp.exp(jax.random.uniform(seeds[2], (LEV_ATM,), jnp.float32, math.log(0.02), math.log(0.15))), 0.02, 0.15)
    ocean_tracers = bell_draw(seeds[3], (2, LEV_OCN, NROWS_OCN, NCOLS), 1.0, 6.0, ((2, 12), (3, 64)))
    ocean_courant = jnp.clip(jax.random.uniform(seeds[4], (LEV_OCN, NROWS_OCN, NCOLS), jnp.float32, -0.5, 0.5) * steps_of(seeds[4], (LEV_OCN, NROWS_OCN, NCOLS), ((1, 12), (2, 64)), -0.4, 0.0), -0.5, 0.5).astype(jnp.bfloat16)
    ocean_diffusion = jnp.clip(jnp.exp(jax.random.uniform(seeds[5], (LEV_OCN,), jnp.float32, math.log(0.02), math.log(0.15))), 0.02, 0.15)
    surface_seen = bell_draw(seeds[6], (2, NROWS_ATM, NCOLS), 1.0, 6.0, ((1, 12), (2, 64)), jnp.float32)
    bulk_coeff = jnp.clip(jnp.exp(math.log(1.0) - 1.609438 * jax.random.uniform(seeds[7], (NROWS_ATM, NCOLS), jnp.float32) ** steps_of(seeds[7], (NROWS_ATM, NCOLS), ((0, 12), (1, 64)), -0.2, 0.2)), 0.2, 1.0)
    flux_owner_keys = jax.random.split(jax.random.fold_in(seeds[8], 1), N_SEC * N_TILE * ROWS_ATM // ROWS_ATM)
    flux_owner_turns = jax.random.permutation(jax.random.fold_in(seeds[8], 3), N_SEC * N_TILE * ROWS_ATM // ROWS_ATM)
    flux_owner = jax.vmap(lambda own, number: assign_block(jax.random.fold_in(seeds[8], 2), own, number, ROWS_ATM, N_SEC, 1, FLUX_CAP, 2))(flux_owner_keys, flux_owner_turns).reshape((N_SEC, N_TILE, ROWS_ATM, 1))
    flux_slot = touch_ends(jax.random.randint(seeds[9], (N_SEC, N_TILE, ROWS_ATM), 0, ROWS_OCN), jax.random.fold_in(seeds[9], 1), 0, ROWS_OCN - 1).astype(jnp.int32)
    flux_weight = jnp.clip(0.5 + 1.0 * jax.random.uniform(seeds[10], (N_SEC, N_TILE, ROWS_ATM), jnp.float32) ** steps_of(seeds[10], (N_SEC, N_TILE, ROWS_ATM), ((0, 12), (1, 64)), -0.2, 0.2), 0.5, 1.5)
    ocean_mask = touch_ends((jax.random.randint(seeds[11], (NROWS_OCN, NCOLS), 0, 4) < 3).astype(jnp.int32), jax.random.fold_in(seeds[11], 1), 0, 1)
    return {"atm_tracers": atm_tracers, "atm_courant": atm_courant, "atm_diffusion": atm_diffusion, "ocean_tracers": ocean_tracers, "ocean_courant": ocean_courant, "ocean_diffusion": ocean_diffusion, "surface_seen": surface_seen, "bulk_coeff": bulk_coeff, "flux_owner": flux_owner, "flux_slot": flux_slot, "flux_weight": flux_weight, "ocean_mask": ocean_mask}


def advance_global(field, speed, diffusion):
    right = jnp.roll(field, -1, axis=-1)
    left = jnp.roll(field, 1, axis=-1)
    transport = -0.5 * speed * (right - left) + 0.5 * speed * speed * (right - 2.0 * field + left)
    upper = jnp.concatenate([field[..., :1, :, :], field[..., :-1, :, :]], axis=-3)
    lower = jnp.concatenate([field[..., 1:, :, :], field[..., -1:, :, :]], axis=-3)
    mixing = diffusion[:, None, None] * (upper - 2.0 * field + lower)
    return field + transport + mixing


def evolve(field, speed_bf, diffusion, count, band_rows):
    levels = field.shape[1]
    columns = field.shape[-1]
    bands = jnp.transpose(field.reshape(2, levels, N_SEC, band_rows, columns), (2, 0, 1, 3, 4))
    speeds = jnp.transpose(speed_bf.reshape(levels, N_SEC, band_rows, columns), (1, 0, 2, 3))

    def one_band(pair):
        state, speed_band = pair
        speed_band = speed_band.astype(jnp.float32)
        for repeat in range(count):
            state = advance_global(state, speed_band, diffusion)
        return state

    result = lax.map(one_band, (bands, speeds))
    return jnp.transpose(result, (1, 2, 0, 3, 4)).reshape(2, levels, N_SEC * band_rows, columns)


def reference(atm_tracers, atm_courant, atm_diffusion, ocean_tracers, ocean_courant, ocean_diffusion, surface_seen, bulk_coeff, flux_owner, flux_slot, flux_weight, ocean_mask):
    atm = atm_tracers.astype(jnp.float32)
    heat = bulk_coeff * (atm[0, -1] - surface_seen[0])
    evap = bulk_coeff * (0.5 * surface_seen[0] - atm[1, -1])
    atm = atm.at[0, -1].add(-0.5 * heat).at[1, -1].add(0.5 * evap)
    weight_rows = jnp.transpose(flux_weight, (0, 2, 1)).reshape(N_SEC * ROWS_ATM, N_TILE)
    weight_full = jnp.repeat(weight_rows, STRIP, axis=1)
    blocks = (jnp.stack([heat, evap]) * weight_full[None]).reshape(2, N_SEC, ROWS_ATM, N_TILE, STRIP)
    owner = jnp.transpose(flux_owner[..., 0], (0, 2, 1)).astype(jnp.int32)
    slot = jnp.transpose(flux_slot, (0, 2, 1)).astype(jnp.int32)
    tile_index = jnp.broadcast_to(jnp.arange(N_TILE, dtype=jnp.int32)[None, None, :], owner.shape)
    received = jnp.zeros((2, N_SEC, ROWS_OCN, N_TILE, STRIP), jnp.float32).at[:, owner, slot, tile_index].add(blocks)
    received = received.reshape(2, N_SEC * ROWS_OCN, N_TILE * STRIP) * ocean_mask.astype(jnp.float32)[None]
    ocean = ocean_tracers.astype(jnp.float32)
    ocean = ocean.at[0, 0].add(0.5 * received[0]).at[1, 0].add(0.5 * received[1])
    atm = evolve(atm, atm_courant, atm_diffusion, ATM_STEPS, ROWS_ATM)
    ocean = evolve(ocean, ocean_courant, ocean_diffusion, OCN_STEPS, ROWS_OCN)
    top = ocean[:, 0].reshape(2, N_SEC, ROWS_OCN, N_TILE, STRIP)
    surface_next = top[:, owner, slot, tile_index].reshape(2, N_SEC * ROWS_ATM, N_TILE * STRIP)
    return atm.astype(jnp.bfloat16), ocean.astype(jnp.bfloat16), surface_next
```

```python
import jax
import jax.numpy as jnp
from jax import lax
from jax.experimental import pallas as pl
from jax.experimental.pallas import tpu as pltpu
from jax.sharding import PartitionSpec as P

ATM_STEPS = 3
OCN_STEPS = 2
SEC = 12
TILE = 64
ROWS = 8
LANES = 128
LA = 128
LO = 80
GROUP = 16
CHUNK = 8
F32 = jnp.float32
BF16 = jnp.bfloat16
MESH = pl.DeviceIdType.MESH

PA, PAC, PO, POC = 0, 2 * LA // GROUP, 3 * LA // GROUP, (3 * LA + 2 * LO) // GROUP
PACKED = (3 * LA + 3 * LO) // GROUP


def lane_ids():
    return lax.broadcasted_iota(jnp.int32, (ROWS, LANES), 1)


def shifted(main, halo, lane):
    rm, rh = pltpu.roll(main, LANES - 1, 1), pltpu.roll(halo, LANES - 1, 1)
    lm, lh = pltpu.roll(main, 1, 1), pltpu.roll(halo, 1, 1)
    last, first = lane == LANES - 1, lane == 0
    return (
        (jnp.where(last, rh, rm), jnp.where(first, lh, lm)),
        (jnp.where(last, rm, rh), jnp.where(first, lm, lh)),
    )


def cell_step(q, up, dn, right, left, c, k):
    twice = 2.0 * q
    transport = (0.5 * c) * (c * ((right + left) - twice) - (right - left))
    return q + transport + k * ((up + dn) - twice)


def level_step(src_m, src_h, f, l, c_m, c_h, k, lane, with_halo):
    m, h = src_m[f, l + 1], src_h[f, l + 1]
    (rm, lm), (rh, lh) = shifted(m, h, lane)
    new_m = cell_step(m, src_m[f, l], src_m[f, l + 2], rm, lm, c_m, k)
    new_h = None
    if with_halo:
        new_h = cell_step(h, src_h[f, l], src_h[f, l + 2], rh, lh, c_h, k)
    return new_m, new_h


def step_levels(src_m, src_h, dst_m, dst_h, cm_ref, ch_ref, k_ref, levels, out=None):
    @pl.loop(0, levels // CHUNK)
    def _(i):
        lane = lane_ids()
        for g in range(CHUNK):
            l = i * CHUNK + g
            c_m = cm_ref[l].astype(F32)
            c_h = ch_ref[l]
            k = k_ref[l]
            for f in range(2):
                new_m, new_h = level_step(
                    src_m, src_h, f, l, c_m, c_h, k, lane, out is None
                )
                if out is None:
                    dst_m[f, l + 1] = new_m
                    dst_h[f, l + 1] = new_h
                else:
                    out[f, l] = new_m.astype(BF16)

    if out is None:
        pad_levels(dst_m, levels)
        pad_levels(dst_h, levels)


def pad_levels(ref, levels):
    for f in range(2):
        ref[f, 0] = ref[f, 1]
        ref[f, levels + 1] = ref[f, levels]


def widen(src, dst, levels):
    @pl.loop(0, levels // CHUNK)
    def _(i):
        for g in range(CHUNK):
            l = i * CHUNK + g
            for f in range(2):
                dst[f, l + 1] = src[f, l].astype(F32)


def pack_edges(read, groups, base, packed):
    @pl.loop(0, groups)
    def _(i):
        part = lane_ids() // 8
        acc = jnp.zeros((ROWS, LANES), F32)
        for j in range(GROUP):
            rolled = pltpu.roll(read(i * GROUP + j), (8 * j + 4) % LANES, 1)
            acc = jnp.where(part == j, rolled, acc)
        packed[base + i] = acc.astype(BF16)


def unpack_edges(store, groups, base, from_left, from_right):
    @pl.loop(0, groups)
    def _(i):
        lane = lane_ids()
        both = jnp.where(
            lane % 8 < 4,
            from_left[base + i].astype(F32),
            from_right[base + i].astype(F32),
        )
        for j in range(GROUP):
            store(i * GROUP + j, pltpu.roll(both, (LANES - 8 * j - 4) % LANES, 1))


def kernel(
    atm_h, acour_h, adiff_h, ocn_h, ocour_h, odiff_h, seen_h, bulk_h, mask_h, meta,
    atm_o, ocn_o, surf_o,
    atm_in, acour, adiff, ocn_in, ocour, odiff, seen, bulk, mask,
    a0m, a0h, a1m, a1h, o0m, o0h, o1m, o1h, acour_e, ocour_e,
    packed, from_left, from_right,
    flux_out, flux_in, reply_out, reply_in, edge_out, edge_left, edge_right,
    in_sem, flux_ss, flux_rs, reply_ss, reply_rs, halo_ss, halo_rs, edge_ss, edge_rs,
):
    sec = lax.axis_index("sec")
    tile = lax.axis_index("tile")
    to_left = (sec, lax.rem(tile + TILE - 1, TILE))
    to_right = (sec, lax.rem(tile + 1, TILE))
    order = sorted(range(1, SEC), key=lambda k: -min(k, SEC - k))

    barrier = pltpu.get_barrier_semaphore()
    for k in order:
        pl.semaphore_signal(
            barrier, inc=1, device_id=(lax.rem(sec + k, SEC), tile), device_id_type=MESH
        )
    for where in (to_left, to_right):
        pl.semaphore_signal(barrier, inc=1, device_id=where, device_id_type=MESH)

    pairs = [
        (atm_h, atm_in), (seen_h, seen), (bulk_h, bulk), (acour_h, acour),
        (ocn_h, ocn_in), (ocour_h, ocour), (mask_h, mask), (adiff_h, adiff),
        (odiff_h, odiff),
    ]
    loads = [
        pltpu.make_async_copy(src, dst, in_sem.at[i]) for i, (src, dst) in enumerate(pairs)
    ]
    for load in loads:
        load.start()

    lane = lane_ids()
    row = lax.broadcasted_iota(jnp.int32, (ROWS, LANES), 0)

    owner_row, owner_lane = meta[0], meta[1]
    earlier = jnp.sum(
        jnp.where((owner_row == owner_lane) & (row < lane % 8), 1.0, 0.0),
        axis=0,
        keepdims=True,
    )
    target = 8.0 * owner_lane[0:1] + 2.0 * (lane[0:1] // 8).astype(F32) + earlier
    target = jnp.where(lane[0:1] < 24, target, -1.0)
    rows_all = lax.broadcasted_iota(jnp.int32, (8 * SEC, LANES), 0)
    placing = jnp.where(rows_all.astype(F32) == target, 1.0, 0.0)

    for load in loads[:3]:
        load.wait()
    top_t = atm_in[0, LA - 1].astype(F32)
    top_q = atm_in[1, LA - 1].astype(F32)
    heat = bulk[...] * (top_t - seen[0])
    evap = bulk[...] * (0.5 * seen[0] - top_q)
    weight = meta[3]
    payload = jnp.concatenate(
        [heat * weight, evap * weight, meta[2] + 1.0, jnp.zeros((LANES - 24, LANES), F32)],
        axis=0,
    )
    outgoing = jnp.dot(
        placing.astype(BF16), payload.astype(BF16), preferred_element_type=F32
    )
    flux_out[...] = outgoing.reshape(SEC, ROWS, LANES).astype(BF16)
    flux_in[sec] = flux_out[sec]

    widen(atm_in, a0m, LA)
    a0m[0, LA] = top_t - 0.5 * heat
    a0m[1, LA] = top_q + 0.5 * evap
    pad_levels(a0m, LA)
    for load in loads[3:]:
        load.wait()
    widen(ocn_in, o0m, LO)
    pad_levels(o0m, LO)
    for f in range(2):
        pack_edges(lambda l, f=f: a0m[f, l + 1], LA // GROUP, PA + f * LA // GROUP, packed)
        pack_edges(lambda l, f=f: o0m[f, l + 1], LO // GROUP, PO + f * LO // GROUP, packed)
    pack_edges(lambda l: acour[l].astype(F32), LA // GROUP, PAC, packed)
    pack_edges(lambda l: ocour[l].astype(F32), LO // GROUP, POC, packed)

    pl.semaphore_wait(barrier, SEC + 1)

    def to_sec(k, src, dst, ss, rs):
        peer = lax.rem(sec + k, SEC)
        return pltpu.make_async_remote_copy(
            src_ref=src.at[peer], dst_ref=dst.at[sec], send_sem=ss.at[k], recv_sem=rs.at[k],
            device_id=(peer, tile), device_id_type=MESH,
        )

    def to_sides(src, at_left, at_right, ss, rs):
        return [
            pltpu.make_async_remote_copy(
                src_ref=src, dst_ref=dst, send_sem=ss.at[i], recv_sem=rs.at[i],
                device_id=where, device_id_type=MESH,
            )
            for i, (dst, where) in enumerate(((at_left, to_right), (at_right, to_left)))
        ]

    fluxes = [to_sec(k, flux_out, flux_in, flux_ss, flux_rs) for k in order]
    for copy in fluxes:
        copy.start()
    halos = to_sides(packed, from_left, from_right, halo_ss, halo_rs)
    for copy in halos:
        copy.start()
    for copy in halos:
        copy.wait()

    def put_a(f):
        def store(l, value):
            a0h[f, l + 1] = value
        return store

    def put_o(f):
        def store(l, value):
            o0h[f, l + 1] = value
        return store

    def put_ac(l, value):
        acour_e[l] = value

    def put_oc(l, value):
        ocour_e[l] = value

    for f in range(2):
        unpack_edges(put_o(f), LO // GROUP, PO + f * LO // GROUP, from_left, from_right)
    unpack_edges(put_oc, LO // GROUP, POC, from_left, from_right)
    pad_levels(o0h, LO)
    step_levels(o0m, o0h, o1m, o1h, ocour, ocour_e, odiff, LO)
    for f in range(2):
        unpack_edges(put_a(f), LA // GROUP, PA + f * LA // GROUP, from_left, from_right)
    unpack_edges(put_ac, LA // GROUP, PAC, from_left, from_right)
    pad_levels(a0h, LA)
    step_levels(a0m, a0h, a1m, a1h, acour, acour_e, adiff, LA)

    for copy in fluxes:
        copy.wait()
    arrived = flux_in[...].astype(F32).reshape(8 * SEC, LANES)
    lane_all = lax.broadcasted_iota(jnp.int32, (8 * SEC, LANES), 1)
    kind = rows_all % 8
    up2 = pltpu.roll(arrived, 8 * SEC - 2, 0)
    up4 = pltpu.roll(arrived, 8 * SEC - 4, 0)
    slot = (lane_all % 8 + 1).astype(F32)
    collect = jnp.where(
        ((kind < 2) & (lane_all < 8) & (up4 == slot))
        | ((kind >= 2) & (kind < 4) & (lane_all >= 8) & (lane_all < 16) & (up2 == slot)),
        1.0,
        0.0,
    )
    received = lax.dot_general(
        collect.astype(BF16), arrived.astype(BF16), (((0,), (0,)), ((), ())),
        preferred_element_type=F32,
    )
    half = 0.5 * mask[...].astype(F32)
    added = [half * received[8 * f : 8 * f + 8] for f in range(2)]
    for f in range(2):
        edge_out[f] = added[f].astype(BF16)
        o0m[f, 1] = o0m[f, 1] + added[f]
        o0m[f, 0] = o0m[f, 1]
    edges = to_sides(edge_out, edge_left, edge_right, edge_ss, edge_rs)
    for copy in edges:
        copy.start()
    for copy in edges:
        copy.wait()
    for f in range(2):
        outer = jnp.where(
            lane < 4,
            edge_right[f].astype(F32),
            jnp.where(lane >= LANES - 4, edge_left[f].astype(F32), 0.0),
        )
        o0h[f, 1] = o0h[f, 1] + outer
        o0h[f, 0] = o0h[f, 1]
    for l in range(2):
        for f in range(2):
            new_m, new_h = level_step(
                o0m, o0h, f, l, ocour[l].astype(F32), ocour_e[l], odiff[l], lane, True
            )
            o1m[f, l + 1] = new_m
            o1h[f, l + 1] = new_h
    tops = []
    for f in range(2):
        o1m[f, 0] = o1m[f, 1]
        top, _ = level_step(
            o1m, o1h, f, 0, ocour[0].astype(F32), ocour_e[0], odiff[0], lane, False
        )
        tops.append(top)
    rows_top = jnp.concatenate(tops + [jnp.zeros((LANES - 16, LANES), F32)], axis=0)
    answers = jnp.dot(collect.astype(BF16), rows_top.astype(BF16), preferred_element_type=F32)
    reply_out[...] = answers.reshape(SEC, ROWS, LANES).astype(BF16)
    replies = [to_sec(k, reply_out, reply_in, reply_ss, reply_rs) for k in order]
    for copy in replies:
        copy.start()
    reply_in[sec] = reply_out[sec]

    step_levels(o1m, o1h, None, None, ocour, ocour_e, odiff, LO, ocn_o)
    step_levels(a1m, a1h, a0m, a0h, acour, acour_e, adiff, LA)
    step_levels(a0m, a0h, None, None, acour, acour_e, adiff, LA, atm_o)

    for copy in replies:
        copy.wait()
    back = reply_in[...].astype(F32).reshape(8 * SEC, LANES)
    surface = lax.dot_general(
        placing.astype(BF16), back.astype(BF16), (((0,), (0,)), ((), ())),
        preferred_element_type=F32,
    )
    surf_o[0] = surface[0:8]
    surf_o[1] = surface[8:16]


def body(
    atm_tracers, atm_courant, atm_diffusion, ocean_tracers, ocean_courant, ocean_diffusion,
    surface_seen, bulk_coeff, flux_owner, flux_slot, flux_weight, ocean_mask,
):
    shape = (ROWS, LANES)
    owner = flux_owner[0, 0, :, 0].astype(F32)
    by_lane = jnp.pad(jnp.tile(owner, 3), (0, LANES - 24), constant_values=-1.0)
    meta = jnp.stack(
        [
            jnp.broadcast_to(owner[:, None], shape),
            jnp.broadcast_to(by_lane[None, :], shape),
            jnp.broadcast_to(flux_slot[0, 0].astype(F32)[:, None], shape),
            jnp.broadcast_to(flux_weight[0, 0][:, None], shape),
        ]
    )
    hbm = pl.BlockSpec(memory_space=pl.ANY)
    vmem = pl.BlockSpec(memory_space=pltpu.VMEM)
    V = pltpu.VMEM
    D = pltpu.SemaphoreType.DMA
    strip_a, strip_o = V((2, LA + 2) + shape, F32), V((2, LO + 2) + shape, F32)
    return pl.pallas_call(
        kernel,
        out_shape=(
            jax.ShapeDtypeStruct((2, LA) + shape, BF16),
            jax.ShapeDtypeStruct((2, LO) + shape, BF16),
            jax.ShapeDtypeStruct((2,) + shape, F32),
        ),
        in_specs=[hbm] * 9 + [vmem],
        out_specs=(vmem, vmem, vmem),
        scratch_shapes=[
            V((2, LA) + shape, BF16), V((LA,) + shape, BF16), pltpu.SMEM((LA,), F32),
            V((2, LO) + shape, BF16), V((LO,) + shape, BF16), pltpu.SMEM((LO,), F32),
            V((2,) + shape, F32), V(shape, F32), V(shape, jnp.int32),
            strip_a, strip_a, strip_a, strip_a, strip_o, strip_o, strip_o, strip_o,
            V((LA,) + shape, F32), V((LO,) + shape, F32),
            V((PACKED,) + shape, BF16), V((PACKED,) + shape, BF16), V((PACKED,) + shape, BF16),
            V((SEC,) + shape, BF16), V((SEC,) + shape, BF16),
            V((SEC,) + shape, BF16), V((SEC,) + shape, BF16),
            V((2,) + shape, BF16), V((2,) + shape, BF16), V((2,) + shape, BF16),
            D((9,)), D((SEC,)), D((SEC,)), D((SEC,)), D((SEC,)),
            D((2,)), D((2,)), D((2,)), D((2,)),
        ],
        compiler_params=pltpu.CompilerParams(collective_id=0, has_side_effects=True),
        name="coupled_window",
    )(
        atm_tracers, atm_courant, atm_diffusion, ocean_tracers, ocean_courant,
        ocean_diffusion, surface_seen, bulk_coeff, ocean_mask, meta,
    )


def solution(mesh):
    placed = (
        P(None, None, "sec", "tile"),
        P(None, "sec", "tile"),
        P(),
        P(None, None, "sec", "tile"),
        P(None, "sec", "tile"),
        P(),
        P(None, "sec", "tile"),
        P("sec", "tile"),
        P("sec", "tile", None, None),
        P("sec", "tile", None),
        P("sec", "tile", None),
        P("sec", "tile"),
    )
    return jax.shard_map(
        body,
        mesh=mesh,
        in_specs=placed,
        out_specs=(
            P(None, None, "sec", "tile"),
            P(None, None, "sec", "tile"),
            P(None, "sec", "tile"),
        ),
        check_vma=False,
    )
```

```python
import jax
import jax.numpy as jnp
from jax import lax
from jax.experimental import pallas as pl
from jax.experimental.pallas import tpu as pltpu
from jax.sharding import PartitionSpec as P

ATM_STEPS = 3
OCN_STEPS = 2
SEC = 12
TILE = 64
ROWS = 8
LANES = 128
LA = 128
LO = 80
GROUP = 16
CHUNK = 8
F32 = jnp.float32
BF16 = jnp.bfloat16
MESH = pl.DeviceIdType.MESH

PA, PAC, PO, POC = 0, 2 * LA // GROUP, 3 * LA // GROUP, (3 * LA + 2 * LO) // GROUP
PACKED = (3 * LA + 3 * LO) // GROUP


def lane_ids():
    return lax.broadcasted_iota(jnp.int32, (ROWS, LANES), 1)


def shifted(main, halo, lane):
    rm, rh = pltpu.roll(main, LANES - 1, 1), pltpu.roll(halo, LANES - 1, 1)
    lm, lh = pltpu.roll(main, 1, 1), pltpu.roll(halo, 1, 1)
    last, first = lane == LANES - 1, lane == 0
    return (
        (jnp.where(last, rh, rm), jnp.where(first, lh, lm)),
        (jnp.where(last, rm, rh), jnp.where(first, lm, lh)),
    )


def cell_step(q, up, dn, right, left, c, k):
    twice = 2.0 * q
    transport = (0.5 * c) * (c * ((right + left) - twice) - (right - left))
    return q + transport + k * ((up + dn) - twice)


def level_step(src_m, src_h, f, l, c_m, c_h, k, lane, with_halo):
    m, h = src_m[f, l + 1], src_h[f, l + 1]
    (rm, lm), (rh, lh) = shifted(m, h, lane)
    new_m = cell_step(m, src_m[f, l], src_m[f, l + 2], rm, lm, c_m, k)
    new_h = None
    if with_halo:
        new_h = cell_step(h, src_h[f, l], src_h[f, l + 2], rh, lh, c_h, k)
    return new_m, new_h


def step_levels(src_m, src_h, dst_m, dst_h, cm_ref, ch_ref, k_ref, levels, out=None):
    @pl.loop(0, levels // CHUNK)
    def _(i):
        lane = lane_ids()
        for g in range(CHUNK):
            l = i * CHUNK + g
            c_m = cm_ref[l].astype(F32)
            c_h = ch_ref[l]
            k = k_ref[l]
            for f in range(2):
                new_m, new_h = level_step(
                    src_m, src_h, f, l, c_m, c_h, k, lane, out is None
                )
                if out is None:
                    dst_m[f, l + 1] = new_m
                    dst_h[f, l + 1] = new_h
                else:
                    out[f, l] = new_m.astype(BF16)

    if out is None:
        pad_levels(dst_m, levels)
        pad_levels(dst_h, levels)


def pad_levels(ref, levels):
    for f in range(2):
        ref[f, 0] = ref[f, 1]
        ref[f, levels + 1] = ref[f, levels]


def widen(src, dst, levels):
    @pl.loop(0, levels // CHUNK)
    def _(i):
        for g in range(CHUNK):
            l = i * CHUNK + g
            for f in range(2):
                dst[f, l + 1] = src[f, l].astype(F32)


def pack_edges(read, groups, base, packed):
    @pl.loop(0, groups)
    def _(i):
        part = lane_ids() // 8
        acc = jnp.zeros((ROWS, LANES), F32)
        for j in range(GROUP):
            rolled = pltpu.roll(read(i * GROUP + j), (8 * j + 4) % LANES, 1)
            acc = jnp.where(part == j, rolled, acc)
        packed[base + i] = acc.astype(BF16)


def unpack_edges(store, groups, base, from_left, from_right):
    @pl.loop(0, groups)
    def _(i):
        lane = lane_ids()
        both = jnp.where(
            lane % 8 < 4,
            from_left[base + i].astype(F32),
            from_right[base + i].astype(F32),
        )
        for j in range(GROUP):
            store(i * GROUP + j, pltpu.roll(both, (LANES - 8 * j - 4) % LANES, 1))


def kernel(
    atm_h, acour_h, adiff_h, ocn_h, ocour_h, odiff_h, seen_h, bulk_h, mask_h,
    owner_h, slot_h, weight_h,
    atm_o, ocn_o, surf_o,
    top_in, atm_in, acour, adiff, ocn_in, ocour, odiff, seen, bulk, mask, owner, slots, weights,
    a0m, a0h, a1m, a1h, o0m, o0h, o1m, o1h, acour_e, ocour_e,
    packed, from_left, from_right,
    flux_out, flux_in, reply_out, reply_in, edge_out, edge_left, edge_right,
    in_sem, flux_ss, flux_rs, reply_ss, reply_rs, halo_ss, halo_rs, edge_ss, edge_rs,
):
    sec = lax.axis_index("sec")
    tile = lax.axis_index("tile")
    to_left = (sec, lax.rem(tile + TILE - 1, TILE))
    to_right = (sec, lax.rem(tile + 1, TILE))
    order = sorted(range(1, SEC), key=lambda k: -min(k, SEC - k))

    barrier = pltpu.get_barrier_semaphore()
    for k in order:
        pl.semaphore_signal(
            barrier, inc=1, device_id=(lax.rem(sec + k, SEC), tile), device_id_type=MESH
        )
    for where in (to_left, to_right):
        pl.semaphore_signal(barrier, inc=1, device_id=where, device_id_type=MESH)

    pairs = [
        (owner_h, owner), (slot_h, slots), (weight_h, weights),
        (atm_h.at[:, LA - 1], top_in), (seen_h, seen), (bulk_h, bulk),
        (atm_h, atm_in), (ocn_h, ocn_in), (acour_h, acour),
        (ocour_h, ocour), (mask_h, mask), (adiff_h, adiff), (odiff_h, odiff),
    ]
    loads = [
        pltpu.make_async_copy(src, dst, in_sem.at[i]) for i, (src, dst) in enumerate(pairs)
    ]
    for load in loads:
        load.start()

    lane = lane_ids()
    row = lax.broadcasted_iota(jnp.int32, (ROWS, LANES), 0)

    for load in loads[:3]:
        load.wait()
    spread = lane < 24
    owner_row = jnp.zeros((ROWS, LANES), jnp.int32)
    owner_lane, slot_row = owner_row, owner_row
    weight = jnp.zeros((ROWS, LANES), F32)
    for b in range(ROWS):
        owner_row = jnp.where(row == b, owner[b], owner_row)
        slot_row = jnp.where(row == b, slots[b], slot_row)
        weight = jnp.where(row == b, weights[b], weight)
        owner_lane = jnp.where(lane % 8 == b, owner[b], owner_lane)
    owner_lane = jnp.where(spread, owner_lane, -1)
    earlier = jnp.sum(
        jnp.where((owner_row == owner_lane) & (row < lane % 8), 1.0, 0.0),
        axis=0,
        keepdims=True,
    )
    target = 8.0 * owner_lane[0:1].astype(F32) + 2.0 * (lane[0:1] // 8).astype(F32) + earlier
    target = jnp.where(lane[0:1] < 24, target, -1.0)
    rows_all = lax.broadcasted_iota(jnp.int32, (8 * SEC, LANES), 0)
    placing = jnp.where(rows_all.astype(F32) == target, 1.0, 0.0)

    for load in loads[3:6]:
        load.wait()
    top_t = top_in[0].astype(F32)
    top_q = top_in[1].astype(F32)
    heat = bulk[...] * (top_t - seen[0])
    evap = bulk[...] * (0.5 * seen[0] - top_q)
    payload = jnp.concatenate(
        [heat * weight, evap * weight, slot_row.astype(F32) + 1.0, jnp.zeros((LANES - 24, LANES), F32)],
        axis=0,
    )
    outgoing = jnp.dot(
        placing.astype(BF16), payload.astype(BF16), preferred_element_type=F32
    )
    flux_out[...] = outgoing.reshape(SEC, ROWS, LANES).astype(BF16)
    flux_in[sec] = flux_out[sec]

    pl.semaphore_wait(barrier, SEC + 1)

    def to_sec(k, src, dst, ss, rs):
        peer = lax.rem(sec + k, SEC)
        return pltpu.make_async_remote_copy(
            src_ref=src.at[peer], dst_ref=dst.at[sec], send_sem=ss.at[k], recv_sem=rs.at[k],
            device_id=(peer, tile), device_id_type=MESH,
        )

    def to_sides(src, at_left, at_right, ss, rs):
        return [
            pltpu.make_async_remote_copy(
                src_ref=src, dst_ref=dst, send_sem=ss.at[i], recv_sem=rs.at[i],
                device_id=where, device_id_type=MESH,
            )
            for i, (dst, where) in enumerate(((at_left, to_right), (at_right, to_left)))
        ]

    fluxes = [to_sec(k, flux_out, flux_in, flux_ss, flux_rs) for k in order]
    for copy in fluxes:
        copy.start()
    loads[6].wait()
    widen(atm_in, a0m, LA)
    a0m[0, LA] = top_t - 0.5 * heat
    a0m[1, LA] = top_q + 0.5 * evap
    pad_levels(a0m, LA)
    for load in loads[7:]:
        load.wait()
    widen(ocn_in, o0m, LO)
    pad_levels(o0m, LO)
    for f in range(2):
        pack_edges(lambda l, f=f: a0m[f, l + 1], LA // GROUP, PA + f * LA // GROUP, packed)
        pack_edges(lambda l, f=f: o0m[f, l + 1], LO // GROUP, PO + f * LO // GROUP, packed)
    pack_edges(lambda l: acour[l].astype(F32), LA // GROUP, PAC, packed)
    pack_edges(lambda l: ocour[l].astype(F32), LO // GROUP, POC, packed)

    halos = to_sides(packed, from_left, from_right, halo_ss, halo_rs)
    for copy in halos:
        copy.start()
    for copy in halos:
        copy.wait()

    def put_a(f):
        def store(l, value):
            a0h[f, l + 1] = value
        return store

    def put_o(f):
        def store(l, value):
            o0h[f, l + 1] = value
        return store

    def put_ac(l, value):
        acour_e[l] = value

    def put_oc(l, value):
        ocour_e[l] = value

    for f in range(2):
        unpack_edges(put_o(f), LO // GROUP, PO + f * LO // GROUP, from_left, from_right)
    unpack_edges(put_oc, LO // GROUP, POC, from_left, from_right)
    pad_levels(o0h, LO)
    step_levels(o0m, o0h, o1m, o1h, ocour, ocour_e, odiff, LO)
    for f in range(2):
        unpack_edges(put_a(f), LA // GROUP, PA + f * LA // GROUP, from_left, from_right)
    unpack_edges(put_ac, LA // GROUP, PAC, from_left, from_right)
    pad_levels(a0h, LA)
    step_levels(a0m, a0h, a1m, a1h, acour, acour_e, adiff, LA)

    for copy in fluxes:
        copy.wait()
    arrived = flux_in[...].astype(F32).reshape(8 * SEC, LANES)
    lane_all = lax.broadcasted_iota(jnp.int32, (8 * SEC, LANES), 1)
    kind = rows_all % 8
    up2 = pltpu.roll(arrived, 8 * SEC - 2, 0)
    up4 = pltpu.roll(arrived, 8 * SEC - 4, 0)
    slot = (lane_all % 8 + 1).astype(F32)
    collect = jnp.where(
        ((kind < 2) & (lane_all < 8) & (up4 == slot))
        | ((kind >= 2) & (kind < 4) & (lane_all >= 8) & (lane_all < 16) & (up2 == slot)),
        1.0,
        0.0,
    )
    received = lax.dot_general(
        collect.astype(BF16), arrived.astype(BF16), (((0,), (0,)), ((), ())),
        preferred_element_type=F32,
    )
    half = 0.5 * mask[...].astype(F32)
    added = [half * received[8 * f : 8 * f + 8] for f in range(2)]
    for f in range(2):
        edge_out[f] = added[f].astype(BF16)
        o0m[f, 1] = o0m[f, 1] + added[f]
        o0m[f, 0] = o0m[f, 1]
    edges = to_sides(edge_out, edge_left, edge_right, edge_ss, edge_rs)
    for copy in edges:
        copy.start()
    for copy in edges:
        copy.wait()
    for f in range(2):
        outer = jnp.where(
            lane < 4,
            edge_right[f].astype(F32),
            jnp.where(lane >= LANES - 4, edge_left[f].astype(F32), 0.0),
        )
        o0h[f, 1] = o0h[f, 1] + outer
        o0h[f, 0] = o0h[f, 1]
    for l in range(2):
        for f in range(2):
            new_m, new_h = level_step(
                o0m, o0h, f, l, ocour[l].astype(F32), ocour_e[l], odiff[l], lane, True
            )
            o1m[f, l + 1] = new_m
            o1h[f, l + 1] = new_h
    tops = []
    for f in range(2):
        o1m[f, 0] = o1m[f, 1]
        top, _ = level_step(
            o1m, o1h, f, 0, ocour[0].astype(F32), ocour_e[0], odiff[0], lane, False
        )
        tops.append(top)
    rows_top = jnp.concatenate(tops + [jnp.zeros((LANES - 16, LANES), F32)], axis=0)
    answers = jnp.dot(collect.astype(BF16), rows_top.astype(BF16), preferred_element_type=F32)
    reply_out[...] = answers.reshape(SEC, ROWS, LANES).astype(BF16)
    replies = [to_sec(k, reply_out, reply_in, reply_ss, reply_rs) for k in order]
    for copy in replies:
        copy.start()
    reply_in[sec] = reply_out[sec]

    step_levels(o1m, o1h, None, None, ocour, ocour_e, odiff, LO, ocn_o)
    step_levels(a1m, a1h, a0m, a0h, acour, acour_e, adiff, LA)
    step_levels(a0m, a0h, None, None, acour, acour_e, adiff, LA, atm_o)

    for copy in replies:
        copy.wait()
    back = reply_in[...].astype(F32).reshape(8 * SEC, LANES)
    surface = lax.dot_general(
        placing.astype(BF16), back.astype(BF16), (((0,), (0,)), ((), ())),
        preferred_element_type=F32,
    )
    surf_o[0] = surface[0:8]
    surf_o[1] = surface[8:16]


def body(
    atm_tracers, atm_courant, atm_diffusion, ocean_tracers, ocean_courant, ocean_diffusion,
    surface_seen, bulk_coeff, flux_owner, flux_slot, flux_weight, ocean_mask,
):
    shape = (ROWS, LANES)
    hbm = pl.BlockSpec(memory_space=pl.ANY)
    vmem = pl.BlockSpec(memory_space=pltpu.VMEM)
    V = pltpu.VMEM
    D = pltpu.SemaphoreType.DMA
    strip_a, strip_o = V((2, LA + 2) + shape, F32), V((2, LO + 2) + shape, F32)
    held = (V((2, LA) + shape, BF16), V((2, LO) + shape, BF16), V((2,) + shape, F32))
    results = pl.pallas_call(
        kernel,
        out_shape=held,
        in_specs=[hbm] * 12,
        out_specs=(vmem, vmem, vmem),
        scratch_shapes=[
            V((2,) + shape, BF16),
            V((2, LA) + shape, BF16), V((LA,) + shape, BF16), pltpu.SMEM((LA,), F32),
            V((2, LO) + shape, BF16), V((LO,) + shape, BF16), pltpu.SMEM((LO,), F32),
            V((2,) + shape, F32), V(shape, F32), V(shape, jnp.int32),
            pltpu.SMEM((ROWS,), jnp.int32), pltpu.SMEM((ROWS,), jnp.int32),
            pltpu.SMEM((ROWS,), F32),
            strip_a, strip_a, strip_a, strip_a, strip_o, strip_o, strip_o, strip_o,
            V((LA,) + shape, F32), V((LO,) + shape, F32),
            V((PACKED,) + shape, BF16), V((PACKED,) + shape, BF16), V((PACKED,) + shape, BF16),
            V((SEC,) + shape, BF16), V((SEC,) + shape, BF16),
            V((SEC,) + shape, BF16), V((SEC,) + shape, BF16),
            V((2,) + shape, BF16), V((2,) + shape, BF16), V((2,) + shape, BF16),
            D((13,)), D((SEC,)), D((SEC,)), D((SEC,)), D((SEC,)),
            D((2,)), D((2,)), D((2,)), D((2,)),
        ],
        compiler_params=pltpu.CompilerParams(collective_id=0, has_side_effects=True),
        name="coupled_window",
    )(
        atm_tracers, atm_courant, atm_diffusion, ocean_tracers, ocean_courant,
        ocean_diffusion, surface_seen, bulk_coeff, ocean_mask,
        flux_owner.reshape(ROWS), flux_slot.reshape(ROWS), flux_weight.reshape(ROWS),
    )
    return pl.pallas_call(
        put_out,
        out_shape=tuple(jax.ShapeDtypeStruct(r.shape, r.dtype) for r in results),
        in_specs=[vmem] * 3,
        out_specs=(hbm, hbm, hbm),
        scratch_shapes=[D((3,))],
        name="put_out",
    )(*[pltpu.with_memory_space_constraint(r, pltpu.VMEM) for r in results])


def put_out(a_ref, o_ref, s_ref, a_out, o_out, s_out, sems):
    copies = [
        pltpu.make_async_copy(src, dst, sems.at[i])
        for i, (src, dst) in enumerate(((a_ref, a_out), (o_ref, o_out), (s_ref, s_out)))
    ]
    for copy in copies:
        copy.start()
    for copy in copies:
        copy.wait()


def solution(mesh):
    placed = (
        P(None, None, "sec", "tile"),
        P(None, "sec", "tile"),
        P(),
        P(None, None, "sec", "tile"),
        P(None, "sec", "tile"),
        P(),
        P(None, "sec", "tile"),
        P("sec", "tile"),
        P("sec", "tile", None, None),
        P("sec", "tile", None),
        P("sec", "tile", None),
        P("sec", "tile"),
    )
    return jax.shard_map(
        body,
        mesh=mesh,
        in_specs=placed,
        out_specs=(
            P(None, None, "sec", "tile"),
            P(None, None, "sec", "tile"),
            P(None, "sec", "tile"),
        ),
        check_vma=False,
    )
```

```python
import jax
import jax.numpy as jnp
from jax import lax
from jax.experimental import pallas as pl
from jax.experimental.pallas import tpu as pltpu
from jax.sharding import PartitionSpec as P

ATM_STEPS = 3
OCN_STEPS = 2
SEC = 12
TILE = 64
ROWS = 8
LANES = 128
LA = 128
LO = 80
GROUP = 16
CHUNK = 16
F32 = jnp.float32
BF16 = jnp.bfloat16
MESH = pl.DeviceIdType.MESH

PA, PAC, PO, POC = 0, 2 * LA // GROUP, 3 * LA // GROUP, (3 * LA + 2 * LO) // GROUP
PACKED = (3 * LA + 3 * LO) // GROUP


def lane_ids():
    return lax.broadcasted_iota(jnp.int32, (ROWS, LANES), 1)


def shifted(main, halo, lane):
    rm, rh = pltpu.roll(main, LANES - 1, 1), pltpu.roll(halo, LANES - 1, 1)
    lm, lh = pltpu.roll(main, 1, 1), pltpu.roll(halo, 1, 1)
    last, first = lane == LANES - 1, lane == 0
    return (
        (jnp.where(last, rh, rm), jnp.where(first, lh, lm)),
        (jnp.where(last, rm, rh), jnp.where(first, lm, lh)),
    )


def cell_step(q, up, dn, right, left, c, k):
    twice = 2.0 * q
    transport = (0.5 * c) * (c * ((right + left) - twice) - (right - left))
    return q + transport + k * ((up + dn) - twice)


def level_step(src_m, src_h, f, l, c_m, c_h, k, lane, with_halo):
    m, h = src_m[f, l + 1], src_h[f, l + 1]
    (rm, lm), (rh, lh) = shifted(m, h, lane)
    new_m = cell_step(m, src_m[f, l], src_m[f, l + 2], rm, lm, c_m, k)
    new_h = None
    if with_halo:
        new_h = cell_step(h, src_h[f, l], src_h[f, l + 2], rh, lh, c_h, k)
    return new_m, new_h


def step_levels(src_m, src_h, dst_m, dst_h, cm_ref, ch_ref, k_ref, levels, out=None):
    @pl.loop(0, levels // CHUNK)
    def _(i):
        lane = lane_ids()
        for g in range(CHUNK):
            l = i * CHUNK + g
            c_m = cm_ref[l].astype(F32)
            c_h = ch_ref[l]
            k = k_ref[l]
            for f in range(2):
                new_m, new_h = level_step(
                    src_m, src_h, f, l, c_m, c_h, k, lane, out is None
                )
                if out is None:
                    dst_m[f, l + 1] = new_m
                    dst_h[f, l + 1] = new_h
                else:
                    out[f, l] = new_m.astype(BF16)

    if out is None:
        pad_levels(dst_m, levels)
        pad_levels(dst_h, levels)


def pad_levels(ref, levels):
    for f in range(2):
        ref[f, 0] = ref[f, 1]
        ref[f, levels + 1] = ref[f, levels]


def widen(src, dst, levels):
    @pl.loop(0, levels // CHUNK)
    def _(i):
        for g in range(CHUNK):
            l = i * CHUNK + g
            for f in range(2):
                dst[f, l + 1] = src[f, l].astype(F32)


def pack_edges(read, groups, base, packed):
    @pl.loop(0, groups)
    def _(i):
        part = lane_ids() // 8
        acc = jnp.zeros((ROWS, LANES), F32)
        for j in range(GROUP):
            rolled = pltpu.roll(read(i * GROUP + j), (8 * j + 4) % LANES, 1)
            acc = jnp.where(part == j, rolled, acc)
        packed[base + i] = acc.astype(BF16)


def unpack_edges(store, groups, base, from_left, from_right):
    @pl.loop(0, groups)
    def _(i):
        lane = lane_ids()
        both = jnp.where(
            lane % 8 < 4,
            from_left[base + i].astype(F32),
            from_right[base + i].astype(F32),
        )
        for j in range(GROUP):
            store(i * GROUP + j, pltpu.roll(both, (LANES - 8 * j - 4) % LANES, 1))


def kernel(
    atm_h, acour_h, adiff_h, ocn_h, ocour_h, odiff_h, seen_h, bulk_h, mask_h,
    owner_h, slot_h, weight_h,
    atm_o, ocn_o, surf_o,
    top_in, atm_in, acour, adiff, ocn_in, ocour, odiff, seen, bulk, mask, owner, slots, weights,
    a0m, a0h, a1m, a1h, o0m, o0h, o1m, o1h, acour_e, ocour_e,
    packed, from_left, from_right,
    flux_out, flux_in, reply_out, reply_in, edge_out, edge_left, edge_right,
    in_sem, flux_ss, flux_rs, reply_ss, reply_rs, halo_ss, halo_rs, edge_ss, edge_rs,
):
    sec = lax.axis_index("sec")
    tile = lax.axis_index("tile")
    to_left = (sec, lax.rem(tile + TILE - 1, TILE))
    to_right = (sec, lax.rem(tile + 1, TILE))
    order = sorted(range(1, SEC), key=lambda k: -min(k, SEC - k))

    barrier = pltpu.get_barrier_semaphore()
    for k in order:
        pl.semaphore_signal(
            barrier, inc=1, device_id=(lax.rem(sec + k, SEC), tile), device_id_type=MESH
        )
    for where in (to_left, to_right):
        pl.semaphore_signal(barrier, inc=1, device_id=where, device_id_type=MESH)

    pairs = [
        (owner_h, owner), (slot_h, slots), (weight_h, weights),
        (atm_h.at[:, LA - 1], top_in), (seen_h, seen), (bulk_h, bulk),
        (atm_h, atm_in), (ocn_h, ocn_in), (acour_h, acour),
        (ocour_h, ocour), (mask_h, mask), (adiff_h, adiff), (odiff_h, odiff),
    ]
    loads = [
        pltpu.make_async_copy(src, dst, in_sem.at[i]) for i, (src, dst) in enumerate(pairs)
    ]
    for load in loads:
        load.start()

    lane = lane_ids()
    row = lax.broadcasted_iota(jnp.int32, (ROWS, LANES), 0)

    for load in loads[:3]:
        load.wait()
    spread = lane < 24
    owner_row = jnp.zeros((ROWS, LANES), jnp.int32)
    owner_lane, slot_row = owner_row, owner_row
    weight = jnp.zeros((ROWS, LANES), F32)
    for b in range(ROWS):
        owner_row = jnp.where(row == b, owner[b], owner_row)
        slot_row = jnp.where(row == b, slots[b], slot_row)
        weight = jnp.where(row == b, weights[b], weight)
        owner_lane = jnp.where(lane % 8 == b, owner[b], owner_lane)
    owner_lane = jnp.where(spread, owner_lane, -1)
    earlier = jnp.sum(
        jnp.where((owner_row == owner_lane) & (row < lane % 8), 1.0, 0.0),
        axis=0,
        keepdims=True,
    )
    target = 8.0 * owner_lane[0:1].astype(F32) + 2.0 * (lane[0:1] // 8).astype(F32) + earlier
    target = jnp.where(lane[0:1] < 24, target, -1.0)
    rows_all = lax.broadcasted_iota(jnp.int32, (8 * SEC, LANES), 0)
    placing = jnp.where(rows_all.astype(F32) == target, 1.0, 0.0)

    for load in loads[3:6]:
        load.wait()
    top_t = top_in[0].astype(F32)
    top_q = top_in[1].astype(F32)
    heat = bulk[...] * (top_t - seen[0])
    evap = bulk[...] * (0.5 * seen[0] - top_q)
    payload = jnp.concatenate(
        [heat * weight, evap * weight, slot_row.astype(F32) + 1.0, jnp.zeros((LANES - 24, LANES), F32)],
        axis=0,
    )
    outgoing = jnp.dot(
        placing.astype(BF16), payload.astype(BF16), preferred_element_type=F32
    )
    flux_out[...] = outgoing.reshape(SEC, ROWS, LANES).astype(BF16)
    flux_in[sec] = flux_out[sec]

    loads[6].wait()
    widen(atm_in, a0m, LA)
    a0m[0, LA] = top_t - 0.5 * heat
    a0m[1, LA] = top_q + 0.5 * evap
    pad_levels(a0m, LA)
    for load in loads[7:]:
        load.wait()
    widen(ocn_in, o0m, LO)
    pad_levels(o0m, LO)
    for f in range(2):
        pack_edges(lambda l, f=f: a0m[f, l + 1], LA // GROUP, PA + f * LA // GROUP, packed)
        pack_edges(lambda l, f=f: o0m[f, l + 1], LO // GROUP, PO + f * LO // GROUP, packed)
    pack_edges(lambda l: acour[l].astype(F32), LA // GROUP, PAC, packed)
    pack_edges(lambda l: ocour[l].astype(F32), LO // GROUP, POC, packed)

    pl.semaphore_wait(barrier, SEC + 1)

    def to_sec(k, src, dst, ss, rs, used):
        peer = lax.rem(sec + k, SEC)
        return pltpu.make_async_remote_copy(
            src_ref=src.at[peer, 0:used], dst_ref=dst.at[sec, 0:used], send_sem=ss.at[k], recv_sem=rs.at[k],
            device_id=(peer, tile), device_id_type=MESH,
        )

    def to_sides(src, at_left, at_right, ss, rs):
        return [
            pltpu.make_async_remote_copy(
                src_ref=src, dst_ref=dst, send_sem=ss.at[i], recv_sem=rs.at[i],
                device_id=where, device_id_type=MESH,
            )
            for i, (dst, where) in enumerate(((at_left, to_right), (at_right, to_left)))
        ]

    fluxes = [to_sec(k, flux_out, flux_in, flux_ss, flux_rs, 6) for k in order]
    for copy in fluxes:
        copy.start()
    halos = to_sides(packed, from_left, from_right, halo_ss, halo_rs)
    for copy in halos:
        copy.start()
    for copy in halos:
        copy.wait()

    def put_a(f):
        def store(l, value):
            a0h[f, l + 1] = value
        return store

    def put_o(f):
        def store(l, value):
            o0h[f, l + 1] = value
        return store

    def put_ac(l, value):
        acour_e[l] = value

    def put_oc(l, value):
        ocour_e[l] = value

    for f in range(2):
        unpack_edges(put_o(f), LO // GROUP, PO + f * LO // GROUP, from_left, from_right)
    unpack_edges(put_oc, LO // GROUP, POC, from_left, from_right)
    pad_levels(o0h, LO)
    step_levels(o0m, o0h, o1m, o1h, ocour, ocour_e, odiff, LO)

    for copy in fluxes:
        copy.wait()
    arrived = flux_in[...].astype(F32).reshape(8 * SEC, LANES)
    arrived = jnp.where(rows_all % 8 < 6, arrived, 0.0)
    lane_all = lax.broadcasted_iota(jnp.int32, (8 * SEC, LANES), 1)
    kind = rows_all % 8
    up2 = pltpu.roll(arrived, 8 * SEC - 2, 0)
    up4 = pltpu.roll(arrived, 8 * SEC - 4, 0)
    slot = (lane_all % 8 + 1).astype(F32)
    collect = jnp.where(
        ((kind < 2) & (lane_all < 8) & (up4 == slot))
        | ((kind >= 2) & (kind < 4) & (lane_all >= 8) & (lane_all < 16) & (up2 == slot)),
        1.0,
        0.0,
    )
    received = lax.dot_general(
        collect.astype(BF16), arrived.astype(BF16), (((0,), (0,)), ((), ())),
        preferred_element_type=F32,
    )
    half = 0.5 * mask[...].astype(F32)
    added = [half * received[8 * f : 8 * f + 8] for f in range(2)]
    for f in range(2):
        edge_out[f] = added[f].astype(BF16)
        o0m[f, 1] = o0m[f, 1] + added[f]
        o0m[f, 0] = o0m[f, 1]
    edges = to_sides(edge_out, edge_left, edge_right, edge_ss, edge_rs)
    for copy in edges:
        copy.start()
    for f in range(2):
        unpack_edges(put_a(f), LA // GROUP, PA + f * LA // GROUP, from_left, from_right)
    unpack_edges(put_ac, LA // GROUP, PAC, from_left, from_right)
    pad_levels(a0h, LA)
    for copy in edges:
        copy.wait()
    for f in range(2):
        outer = jnp.where(
            lane < 4,
            edge_right[f].astype(F32),
            jnp.where(lane >= LANES - 4, edge_left[f].astype(F32), 0.0),
        )
        o0h[f, 1] = o0h[f, 1] + outer
        o0h[f, 0] = o0h[f, 1]
    for l in range(2):
        for f in range(2):
            new_m, new_h = level_step(
                o0m, o0h, f, l, ocour[l].astype(F32), ocour_e[l], odiff[l], lane, True
            )
            o1m[f, l + 1] = new_m
            o1h[f, l + 1] = new_h
    tops = []
    for f in range(2):
        o1m[f, 0] = o1m[f, 1]
        top, _ = level_step(
            o1m, o1h, f, 0, ocour[0].astype(F32), ocour_e[0], odiff[0], lane, False
        )
        tops.append(top)
    rows_top = jnp.concatenate(tops + [jnp.zeros((LANES - 16, LANES), F32)], axis=0)
    answers = jnp.dot(collect.astype(BF16), rows_top.astype(BF16), preferred_element_type=F32)
    reply_out[...] = answers.reshape(SEC, ROWS, LANES).astype(BF16)
    replies = [to_sec(k, reply_out, reply_in, reply_ss, reply_rs, 4) for k in order]
    for copy in replies:
        copy.start()
    reply_in[sec] = reply_out[sec]

    step_levels(o1m, o1h, None, None, ocour, ocour_e, odiff, LO, ocn_o)
    step_levels(a0m, a0h, a1m, a1h, acour, acour_e, adiff, LA)
    step_levels(a1m, a1h, a0m, a0h, acour, acour_e, adiff, LA)
    step_levels(a0m, a0h, None, None, acour, acour_e, adiff, LA, atm_o)

    for copy in replies:
        copy.wait()
    back = reply_in[...].astype(F32).reshape(8 * SEC, LANES)
    back = jnp.where(kind < 4, back, 0.0)
    surface = lax.dot_general(
        placing.astype(BF16), back.astype(BF16), (((0,), (0,)), ((), ())),
        preferred_element_type=F32,
    )
    surf_o[0] = surface[0:8]
    surf_o[1] = surface[8:16]


def body(
    atm_tracers, atm_courant, atm_diffusion, ocean_tracers, ocean_courant, ocean_diffusion,
    surface_seen, bulk_coeff, flux_owner, flux_slot, flux_weight, ocean_mask,
):
    shape = (ROWS, LANES)
    hbm = pl.BlockSpec(memory_space=pl.ANY)
    vmem = pl.BlockSpec(memory_space=pltpu.VMEM)
    V = pltpu.VMEM
    D = pltpu.SemaphoreType.DMA
    strip_a, strip_o = V((2, LA + 2) + shape, F32), V((2, LO + 2) + shape, F32)
    held = (V((2, LA) + shape, BF16), V((2, LO) + shape, BF16), V((2,) + shape, F32))
    results = pl.pallas_call(
        kernel,
        out_shape=held,
        in_specs=[hbm] * 12,
        out_specs=(vmem, vmem, vmem),
        scratch_shapes=[
            V((2,) + shape, BF16),
            V((2, LA) + shape, BF16), V((LA,) + shape, BF16), pltpu.SMEM((LA,), F32),
            V((2, LO) + shape, BF16), V((LO,) + shape, BF16), pltpu.SMEM((LO,), F32),
            V((2,) + shape, F32), V(shape, F32), V(shape, jnp.int32),
            pltpu.SMEM((ROWS,), jnp.int32), pltpu.SMEM((ROWS,), jnp.int32),
            pltpu.SMEM((ROWS,), F32),
            strip_a, strip_a, strip_a, strip_a, strip_o, strip_o, strip_o, strip_o,
            V((LA,) + shape, F32), V((LO,) + shape, F32),
            V((PACKED,) + shape, BF16), V((PACKED,) + shape, BF16), V((PACKED,) + shape, BF16),
            V((SEC,) + shape, BF16), V((SEC,) + shape, BF16),
            V((SEC,) + shape, BF16), V((SEC,) + shape, BF16),
            V((2,) + shape, BF16), V((2,) + shape, BF16), V((2,) + shape, BF16),
            D((13,)), D((SEC,)), D((SEC,)), D((SEC,)), D((SEC,)),
            D((2,)), D((2,)), D((2,)), D((2,)),
        ],
        compiler_params=pltpu.CompilerParams(collective_id=0, has_side_effects=True),
        name="coupled_window",
    )(
        atm_tracers, atm_courant, atm_diffusion, ocean_tracers, ocean_courant,
        ocean_diffusion, surface_seen, bulk_coeff, ocean_mask,
        flux_owner.reshape(ROWS), flux_slot.reshape(ROWS), flux_weight.reshape(ROWS),
    )
    return pl.pallas_call(
        put_out,
        out_shape=tuple(jax.ShapeDtypeStruct(r.shape, r.dtype) for r in results),
        in_specs=[vmem] * 3,
        out_specs=(hbm, hbm, hbm),
        scratch_shapes=[D((3,))],
        name="put_out",
    )(*[pltpu.with_memory_space_constraint(r, pltpu.VMEM) for r in results])


def put_out(a_ref, o_ref, s_ref, a_out, o_out, s_out, sems):
    copies = [
        pltpu.make_async_copy(src, dst, sems.at[i])
        for i, (src, dst) in enumerate(((a_ref, a_out), (o_ref, o_out), (s_ref, s_out)))
    ]
    for copy in copies:
        copy.start()
    for copy in copies:
        copy.wait()


def solution(mesh):
    placed = (
        P(None, None, "sec", "tile"),
        P(None, "sec", "tile"),
        P(),
        P(None, None, "sec", "tile"),
        P(None, "sec", "tile"),
        P(),
        P(None, "sec", "tile"),
        P("sec", "tile"),
        P("sec", "tile", None, None),
        P("sec", "tile", None),
        P("sec", "tile", None),
        P("sec", "tile"),
    )
    return jax.shard_map(
        body,
        mesh=mesh,
        in_specs=placed,
        out_specs=(
            P(None, None, "sec", "tile"),
            P(None, None, "sec", "tile"),
            P(None, "sec", "tile"),
        ),
        check_vma=False,
    )
```

```python
import jax
import jax.numpy as jnp
from jax import lax
from jax.experimental import pallas as pl
from jax.experimental.pallas import tpu as pltpu
from jax.sharding import PartitionSpec as P

ATM_STEPS = 3
OCN_STEPS = 2
SEC = 12
TILE = 64
ROWS = 8
LANES = 128
LA = 128
LO = 80
GROUP = 16
CHUNK = 16
F32 = jnp.float32
BF16 = jnp.bfloat16
MESH = pl.DeviceIdType.MESH

PO, POC, PACKED = 0, 2 * LO // GROUP, 3 * LO // GROUP
WIN = 16
PER = LANES // WIN
GA = LA // PER


def lane_ids():
    return lax.broadcasted_iota(jnp.int32, (ROWS, LANES), 1)


def shifted(main, halo, lane):
    rm, rh = pltpu.roll(main, LANES - 1, 1), pltpu.roll(halo, LANES - 1, 1)
    lm, lh = pltpu.roll(main, 1, 1), pltpu.roll(halo, 1, 1)
    last, first = lane == LANES - 1, lane == 0
    return (
        (jnp.where(last, rh, rm), jnp.where(first, lh, lm)),
        (jnp.where(last, rm, rh), jnp.where(first, lm, lh)),
    )


def cell_step(q, up, dn, right, left, c, k):
    twice = 2.0 * q
    transport = (0.5 * c) * (c * ((right + left) - twice) - (right - left))
    return q + transport + k * ((up + dn) - twice)


def level_step(src_m, src_h, f, l, c_m, c_h, k, lane, with_halo):
    m, h = src_m[f, l + 1], src_h[f, l + 1]
    (rm, lm), (rh, lh) = shifted(m, h, lane)
    new_m = cell_step(m, src_m[f, l], src_m[f, l + 2], rm, lm, c_m, k)
    new_h = None
    if with_halo:
        new_h = cell_step(h, src_h[f, l], src_h[f, l + 2], rh, lh, c_h, k)
    return new_m, new_h


def step_levels(src_m, src_h, dst_m, dst_h, cm_ref, ch_ref, k_ref, levels, out=None):
    @pl.loop(0, levels // CHUNK)
    def _(i):
        lane = lane_ids()
        for g in range(CHUNK):
            l = i * CHUNK + g
            c_m = cm_ref[l].astype(F32)
            c_h = ch_ref[l]
            k = k_ref[l]
            for f in range(2):
                new_m, new_h = level_step(
                    src_m, src_h, f, l, c_m, c_h, k, lane, out is None
                )
                if out is None:
                    dst_m[f, l + 1] = new_m
                    dst_h[f, l + 1] = new_h
                else:
                    out[f, l] = new_m.astype(BF16)

    if out is None:
        pad_levels(dst_m, levels)
        pad_levels(dst_h, levels)


def pad_levels(ref, levels):
    for f in range(2):
        ref[f, 0] = ref[f, 1]
        ref[f, levels + 1] = ref[f, levels]


def widen(src, dst, levels):
    @pl.loop(0, levels // CHUNK)
    def _(i):
        for g in range(CHUNK):
            l = i * CHUNK + g
            for f in range(2):
                dst[f, l + 1] = src[f, l].astype(F32)


def pack_edges(read, groups, base, packed):
    @pl.loop(0, groups)
    def _(i):
        part = lane_ids() // 8
        acc = jnp.zeros((ROWS, LANES), F32)
        for j in range(GROUP):
            rolled = pltpu.roll(read(i * GROUP + j), (8 * j + 4) % LANES, 1)
            acc = jnp.where(part == j, rolled, acc)
        packed[base + i] = acc.astype(BF16)


def unpack_edges(store, groups, base, from_left, from_right):
    @pl.loop(0, groups)
    def _(i):
        lane = lane_ids()
        both = jnp.where(
            lane % 8 < 4,
            from_left[base + i].astype(F32),
            from_right[base + i].astype(F32),
        )
        for j in range(GROUP):
            store(i * GROUP + j, pltpu.roll(both, (LANES - 8 * j - 4) % LANES, 1))


def strip_steps(src, dst, c_ref, k_ref, levels):
    @pl.loop(0, levels // CHUNK)
    def _(i):
        for g in range(CHUNK):
            l = i * CHUNK + g
            c = c_ref[l].astype(F32)
            k = k_ref[l]
            for f in range(2):
                m = src[f, l + 1]
                right, left = pltpu.roll(m, LANES - 1, 1), pltpu.roll(m, 1, 1)
                dst[f, l + 1] = cell_step(m, src[f, l], src[f, l + 2], right, left, c, k)

    pad_levels(dst, levels)


def pack_windows(read, base, wide):
    @pl.loop(0, GA // 2)
    def _(i):
        part = lane_ids() // WIN
        for h in range(2):
            acc = jnp.zeros((ROWS, LANES), F32)
            for j in range(PER):
                shift = (WIN * j + WIN // 2) % LANES
                rolled = pltpu.roll(read((2 * i + h) * PER + j), shift, 1)
                acc = jnp.where(part == j, rolled, acc)
            wide[base + 2 * i + h] = acc.astype(BF16)


def pad_seams(ref):
    for x in range(2):
        for f in range(2):
            ref[x, f, 0] = pltpu.roll(ref[x, f, 1], LANES - WIN, 1)
            ref[x, f, GA + 1] = pltpu.roll(ref[x, f, GA], WIN, 1)


def open_seams(wide, wide_left, wide_right, seams, speeds, k_ref, k_tiles):
    @pl.loop(0, GA)
    def _(i):
        lane = lane_ids()
        first = lane % WIN < WIN // 2
        for n in range(3):
            own = wide[n * GA + i].astype(F32)
            at_left = jnp.where(first, wide_left[n * GA + i].astype(F32), own)
            at_right = jnp.where(first, own, wide_right[n * GA + i].astype(F32))
            if n < 2:
                seams[0, n, i + 1] = at_left
                seams[1, n, i + 1] = at_right
            else:
                speeds[0, i] = at_left
                speeds[1, i] = at_right
        k = jnp.zeros((ROWS, LANES), F32)
        for j in range(PER):
            k = jnp.where(lane // WIN == j, k_ref[i * PER + j], k)
        k_tiles[i] = k

    pad_seams(seams)


def seam_steps(src, dst, speeds, k_tiles):
    @pl.loop(0, GA // 2)
    def _(h):
        lane = lane_ids()
        for i in (2 * h, 2 * h + 1):
            k = k_tiles[i]
            for x in range(2):
                c = speeds[x, i]
                for f in range(2):
                    q = src[x, f, i + 1]
                    above = jnp.where(lane >= LANES - WIN, src[x, f, i], q)
                    below = jnp.where(lane < WIN, src[x, f, i + 2], q)
                    dst[x, f, i + 1] = cell_step(
                        q, pltpu.roll(above, WIN, 1), pltpu.roll(below, LANES - WIN, 1),
                        pltpu.roll(q, LANES - 1, 1), pltpu.roll(q, 1, 1), c, k,
                    )

    pad_seams(dst)


def close_seams(strip, seams, out):
    @pl.loop(0, GA)
    def _(i):
        lane = lane_ids()
        edge = (lane < ATM_STEPS) | (lane >= LANES - ATM_STEPS)
        for f in range(2):
            own = jnp.where(lane % WIN < WIN // 2, seams[1, f, i + 1], seams[0, f, i + 1])
            for j in range(PER):
                l = i * PER + j
                rolled = pltpu.roll(own, (LANES - WIN * j - WIN // 2) % LANES, 1)
                out[f, l] = jnp.where(edge, rolled, strip[f, l + 1]).astype(BF16)


def kernel(
    atm_h, acour_h, adiff_h, ocn_h, ocour_h, odiff_h, seen_h, bulk_h, mask_h,
    owner_h, slot_h, weight_h,
    atm_o, ocn_o, surf_o,
    top_in, atm_in, acour, adiff, ocn_in, ocour, odiff, seen, bulk, mask, owner, slots, weights,
    a0m, a1m, o0m, o0h, o1m, o1h, ocour_e, seam0, seam1, speeds, k_tiles,
    packed, from_left, from_right, wide, wide_left, wide_right,
    flux_out, flux_in, reply_out, reply_in, edge_out, edge_left, edge_right,
    in_sem, flux_ss, flux_rs, reply_ss, reply_rs, halo_ss, halo_rs, wide_ss, wide_rs, edge_ss, edge_rs,
):
    sec = lax.axis_index("sec")
    tile = lax.axis_index("tile")
    to_left = (sec, lax.rem(tile + TILE - 1, TILE))
    to_right = (sec, lax.rem(tile + 1, TILE))
    order = sorted(range(1, SEC), key=lambda k: -min(k, SEC - k))

    barrier = pltpu.get_barrier_semaphore()
    for k in order:
        pl.semaphore_signal(
            barrier, inc=1, device_id=(lax.rem(sec + k, SEC), tile), device_id_type=MESH
        )
    for where in (to_left, to_right):
        pl.semaphore_signal(barrier, inc=1, device_id=where, device_id_type=MESH)

    pairs = [
        (owner_h, owner), (slot_h, slots), (weight_h, weights),
        (atm_h.at[:, LA - 1], top_in), (seen_h, seen), (bulk_h, bulk),
        (atm_h, atm_in), (ocn_h, ocn_in), (acour_h, acour),
        (ocour_h, ocour), (mask_h, mask), (adiff_h, adiff), (odiff_h, odiff),
    ]
    loads = [
        pltpu.make_async_copy(src, dst, in_sem.at[i]) for i, (src, dst) in enumerate(pairs)
    ]
    for load in loads:
        load.start()

    lane = lane_ids()
    row = lax.broadcasted_iota(jnp.int32, (ROWS, LANES), 0)

    for load in loads[:3]:
        load.wait()
    spread = lane < 24
    owner_row = jnp.zeros((ROWS, LANES), jnp.int32)
    owner_lane, slot_row = owner_row, owner_row
    weight = jnp.zeros((ROWS, LANES), F32)
    for b in range(ROWS):
        owner_row = jnp.where(row == b, owner[b], owner_row)
        slot_row = jnp.where(row == b, slots[b], slot_row)
        weight = jnp.where(row == b, weights[b], weight)
        owner_lane = jnp.where(lane % 8 == b, owner[b], owner_lane)
    owner_lane = jnp.where(spread, owner_lane, -1)
    earlier = jnp.sum(
        jnp.where((owner_row == owner_lane) & (row < lane % 8), 1.0, 0.0),
        axis=0,
        keepdims=True,
    )
    target = 8.0 * owner_lane[0:1].astype(F32) + 2.0 * (lane[0:1] // 8).astype(F32) + earlier
    target = jnp.where(lane[0:1] < 24, target, -1.0)
    rows_all = lax.broadcasted_iota(jnp.int32, (8 * SEC, LANES), 0)
    placing = jnp.where(rows_all.astype(F32) == target, 1.0, 0.0)

    for load in loads[3:6]:
        load.wait()
    top_t = top_in[0].astype(F32)
    top_q = top_in[1].astype(F32)
    heat = bulk[...] * (top_t - seen[0])
    evap = bulk[...] * (0.5 * seen[0] - top_q)
    payload = jnp.concatenate(
        [heat * weight, evap * weight, slot_row.astype(F32) + 1.0, jnp.zeros((LANES - 24, LANES), F32)],
        axis=0,
    )
    outgoing = jnp.dot(
        placing.astype(BF16), payload.astype(BF16), preferred_element_type=F32
    )
    flux_out[...] = outgoing.reshape(SEC, ROWS, LANES).astype(BF16)
    flux_in[sec] = flux_out[sec]

    loads[6].wait()
    widen(atm_in, a0m, LA)
    a0m[0, LA] = top_t - 0.5 * heat
    a0m[1, LA] = top_q + 0.5 * evap
    pad_levels(a0m, LA)
    for load in loads[7:]:
        load.wait()
    widen(ocn_in, o0m, LO)
    pad_levels(o0m, LO)
    for f in range(2):
        pack_windows(lambda l, f=f: a0m[f, l + 1], f * GA, wide)
        pack_edges(lambda l, f=f: o0m[f, l + 1], LO // GROUP, PO + f * LO // GROUP, packed)
    pack_windows(lambda l: acour[l].astype(F32), 2 * GA, wide)
    pack_edges(lambda l: ocour[l].astype(F32), LO // GROUP, POC, packed)

    pl.semaphore_wait(barrier, SEC + 1)

    def to_sec(k, src, dst, ss, rs, used):
        peer = lax.rem(sec + k, SEC)
        return pltpu.make_async_remote_copy(
            src_ref=src.at[peer, 0:used], dst_ref=dst.at[sec, 0:used], send_sem=ss.at[k], recv_sem=rs.at[k],
            device_id=(peer, tile), device_id_type=MESH,
        )

    def to_sides(src, at_left, at_right, ss, rs):
        return [
            pltpu.make_async_remote_copy(
                src_ref=src, dst_ref=dst, send_sem=ss.at[i], recv_sem=rs.at[i],
                device_id=where, device_id_type=MESH,
            )
            for i, (dst, where) in enumerate(((at_left, to_right), (at_right, to_left)))
        ]

    fluxes = [to_sec(k, flux_out, flux_in, flux_ss, flux_rs, 6) for k in order]
    for copy in fluxes:
        copy.start()
    halos = to_sides(packed, from_left, from_right, halo_ss, halo_rs)
    for copy in halos:
        copy.start()
    sides = to_sides(wide, wide_left, wide_right, wide_ss, wide_rs)
    for copy in sides:
        copy.start()
    strip_steps(a0m, a1m, acour, adiff, LA)
    strip_steps(a1m, a0m, acour, adiff, LA)
    strip_steps(a0m, a1m, acour, adiff, LA)
    for copy in halos:
        copy.wait()

    def put_o(f):
        def store(l, value):
            o0h[f, l + 1] = value
        return store

    def put_oc(l, value):
        ocour_e[l] = value

    for f in range(2):
        unpack_edges(put_o(f), LO // GROUP, PO + f * LO // GROUP, from_left, from_right)
    unpack_edges(put_oc, LO // GROUP, POC, from_left, from_right)
    pad_levels(o0h, LO)

    for copy in fluxes:
        copy.wait()
    arrived = flux_in[...].astype(F32).reshape(8 * SEC, LANES)
    arrived = jnp.where(rows_all % 8 < 6, arrived, 0.0)
    lane_all = lax.broadcasted_iota(jnp.int32, (8 * SEC, LANES), 1)
    kind = rows_all % 8
    up2 = pltpu.roll(arrived, 8 * SEC - 2, 0)
    up4 = pltpu.roll(arrived, 8 * SEC - 4, 0)
    slot = (lane_all % 8 + 1).astype(F32)
    collect = jnp.where(
        ((kind < 2) & (lane_all < 8) & (up4 == slot))
        | ((kind >= 2) & (kind < 4) & (lane_all >= 8) & (lane_all < 16) & (up2 == slot)),
        1.0,
        0.0,
    )
    received = lax.dot_general(
        collect.astype(BF16), arrived.astype(BF16), (((0,), (0,)), ((), ())),
        preferred_element_type=F32,
    )
    half = 0.5 * mask[...].astype(F32)
    added = [half * received[8 * f : 8 * f + 8] for f in range(2)]
    for f in range(2):
        edge_out[f] = added[f].astype(BF16)
        o0m[f, 1] = o0m[f, 1] + added[f]
        o0m[f, 0] = o0m[f, 1]
    edges = to_sides(edge_out, edge_left, edge_right, edge_ss, edge_rs)
    for copy in edges:
        copy.start()
    step_levels(o0m, o0h, o1m, o1h, ocour, ocour_e, odiff, LO)
    for copy in edges:
        copy.wait()
    for f in range(2):
        outer = jnp.where(
            lane < 4,
            edge_right[f].astype(F32),
            jnp.where(lane >= LANES - 4, edge_left[f].astype(F32), 0.0),
        )
        o0h[f, 1] = o0h[f, 1] + outer
        o0h[f, 0] = o0h[f, 1]
    for l in range(2):
        for f in range(2):
            new_m, new_h = level_step(
                o0m, o0h, f, l, ocour[l].astype(F32), ocour_e[l], odiff[l], lane, True
            )
            o1m[f, l + 1] = new_m
            o1h[f, l + 1] = new_h
    tops = []
    for f in range(2):
        o1m[f, 0] = o1m[f, 1]
        top, _ = level_step(
            o1m, o1h, f, 0, ocour[0].astype(F32), ocour_e[0], odiff[0], lane, False
        )
        tops.append(top)
    rows_top = jnp.concatenate(tops + [jnp.zeros((LANES - 16, LANES), F32)], axis=0)
    answers = jnp.dot(collect.astype(BF16), rows_top.astype(BF16), preferred_element_type=F32)
    reply_out[...] = answers.reshape(SEC, ROWS, LANES).astype(BF16)
    replies = [to_sec(k, reply_out, reply_in, reply_ss, reply_rs, 4) for k in order]
    for copy in replies:
        copy.start()
    reply_in[sec] = reply_out[sec]

    step_levels(o1m, o1h, None, None, ocour, ocour_e, odiff, LO, ocn_o)
    for copy in sides:
        copy.wait()
    open_seams(wide, wide_left, wide_right, seam0, speeds, adiff, k_tiles)
    seam_steps(seam0, seam1, speeds, k_tiles)
    seam_steps(seam1, seam0, speeds, k_tiles)
    seam_steps(seam0, seam1, speeds, k_tiles)
    close_seams(a1m, seam1, atm_o)
    for copy in replies:
        copy.wait()
    back = reply_in[...].astype(F32).reshape(8 * SEC, LANES)
    back = jnp.where(kind < 4, back, 0.0)
    surface = lax.dot_general(
        placing.astype(BF16), back.astype(BF16), (((0,), (0,)), ((), ())),
        preferred_element_type=F32,
    )
    surf_o[0] = surface[0:8]
    surf_o[1] = surface[8:16]


def body(
    atm_tracers, atm_courant, atm_diffusion, ocean_tracers, ocean_courant, ocean_diffusion,
    surface_seen, bulk_coeff, flux_owner, flux_slot, flux_weight, ocean_mask,
):
    shape = (ROWS, LANES)
    hbm = pl.BlockSpec(memory_space=pl.ANY)
    vmem = pl.BlockSpec(memory_space=pltpu.VMEM)
    V = pltpu.VMEM
    D = pltpu.SemaphoreType.DMA
    seam = V((2, 2, GA + 2) + shape, F32)
    strip_a, strip_o = V((2, LA + 2) + shape, F32), V((2, LO + 2) + shape, F32)
    held = (V((2, LA) + shape, BF16), V((2, LO) + shape, BF16), V((2,) + shape, F32))
    results = pl.pallas_call(
        kernel,
        out_shape=held,
        in_specs=[hbm] * 12,
        out_specs=(vmem, vmem, vmem),
        scratch_shapes=[
            V((2,) + shape, BF16),
            V((2, LA) + shape, BF16), V((LA,) + shape, BF16), pltpu.SMEM((LA,), F32),
            V((2, LO) + shape, BF16), V((LO,) + shape, BF16), pltpu.SMEM((LO,), F32),
            V((2,) + shape, F32), V(shape, F32), V(shape, jnp.int32),
            pltpu.SMEM((ROWS,), jnp.int32), pltpu.SMEM((ROWS,), jnp.int32),
            pltpu.SMEM((ROWS,), F32),
            strip_a, strip_a, strip_o, strip_o, strip_o, strip_o, V((LO,) + shape, F32),
            seam, seam, V((2, GA) + shape, F32), V((GA,) + shape, F32),
            V((PACKED,) + shape, BF16), V((PACKED,) + shape, BF16), V((PACKED,) + shape, BF16),
            V((3 * GA,) + shape, BF16), V((3 * GA,) + shape, BF16), V((3 * GA,) + shape, BF16),
            V((SEC,) + shape, BF16), V((SEC,) + shape, BF16),
            V((SEC,) + shape, BF16), V((SEC,) + shape, BF16),
            V((2,) + shape, BF16), V((2,) + shape, BF16), V((2,) + shape, BF16),
            D((13,)), D((SEC,)), D((SEC,)), D((SEC,)), D((SEC,)),
            D((2,)), D((2,)), D((2,)), D((2,)), D((2,)), D((2,)),
        ],
        compiler_params=pltpu.CompilerParams(collective_id=0, has_side_effects=True),
        name="coupled_window",
    )(
        atm_tracers, atm_courant, atm_diffusion, ocean_tracers, ocean_courant,
        ocean_diffusion, surface_seen, bulk_coeff, ocean_mask,
        flux_owner.reshape(ROWS), flux_slot.reshape(ROWS), flux_weight.reshape(ROWS),
    )
    return pl.pallas_call(
        put_out,
        out_shape=tuple(jax.ShapeDtypeStruct(r.shape, r.dtype) for r in results),
        in_specs=[vmem] * 3,
        out_specs=(hbm, hbm, hbm),
        scratch_shapes=[D((3,))],
        name="put_out",
    )(*[pltpu.with_memory_space_constraint(r, pltpu.VMEM) for r in results])


def put_out(a_ref, o_ref, s_ref, a_out, o_out, s_out, sems):
    copies = [
        pltpu.make_async_copy(src, dst, sems.at[i])
        for i, (src, dst) in enumerate(((a_ref, a_out), (o_ref, o_out), (s_ref, s_out)))
    ]
    for copy in copies:
        copy.start()
    for copy in copies:
        copy.wait()


def solution(mesh):
    placed = (
        P(None, None, "sec", "tile"),
        P(None, "sec", "tile"),
        P(),
        P(None, None, "sec", "tile"),
        P(None, "sec", "tile"),
        P(),
        P(None, "sec", "tile"),
        P("sec", "tile"),
        P("sec", "tile", None, None),
        P("sec", "tile", None),
        P("sec", "tile", None),
        P("sec", "tile"),
    )
    return jax.shard_map(
        body,
        mesh=mesh,
        in_specs=placed,
        out_specs=(
            P(None, None, "sec", "tile"),
            P(None, None, "sec", "tile"),
            P(None, "sec", "tile"),
        ),
        check_vma=False,
    )
```
